768 devices in a mesh: grp: 8 (over y_hi, core), tp: 8 (over y_lo, x), seq: 12 (over z).
Axes of the slice: x: 4, y: 8 (y_hi: 4, y_lo: 2; y = y_hi * 2 + y_lo), z: 12, core: 2. Of those that a mesh axis runs over, the one named last changes fastest.
Arguments:
- crops: bfloat16 [8, 12, 576, 1024], P('grp', 'seq', 'tp'), may hold values from -6 to 6
- dout: bfloat16 [8, 12, 576, 1024], P('grp', 'seq', None, 'tp'), may hold values from -0.796875 to 0.796875
- crop_count: int32 [8], P('grp'), may hold values from 4 to 12, as said below
- crop_ids: int32 [8, 12], P('grp'), may hold values from 0 to 11, each once within a row
- seq_slot: int32 [8, 12], P('grp'), may hold values from 0 to 11, as said below
- norm_gain: bfloat16 [1024], replicated, may hold values from 0.099609375 to 1.8984375
- qkv_weight: bfloat16 [3, 1024, 1024], P(None, None, 'tp'), may hold values from -40 to 40
Outputs:
- weight_grad: float32 [3072, 1024], P(('grp', 'seq'), 'tp')
The draws below stay inside these ranges and needn't reach their ends.
Inputs may be any that keep to these rules, and one draw needn't show every extreme that they name: `crop_count`: some page selects 12 crops. `seq_slot`: distinct within a row; only the first crop_count entries of a row are used. `crop_ids`: only the first crop_count entries of a row are used.
All inputs are finite; a program needn't handle non-finite values.
Results may differ from the reference program's by a relative error of at most 0.0084.
Values may be sent and summed in bfloat16 or wider, within the bound.
No kernel may reach another device: no remote copies, remote signals or barrier semaphores. Data moves between devices by JAX's collectives and lax.ppermute only.
A program may use at most 32 MiB of HBM per device.

```python
import jax
import jax.numpy as jnp
from jax import lax

DV = 1024
HEADS = 16
HD = 64
CTOK = 576
SELMAX = 12
SLOTS = 12
PAGES = 8


def draw_crop_count(key, part):
    counts = jax.random.randint(key, (PAGES,), (SELMAX + 2) // 3, SELMAX + 1)
    full_page = jax.random.randint(jax.random.fold_in(key, 7), (), 0, PAGES)
    return jnp.where(jnp.arange(PAGES) == full_page, SELMAX, counts).astype(jnp.int32)


def slot_row(page_key):
    return jax.random.permutation(page_key, SLOTS)[:SELMAX]


def draw_seq_slot(key, part):
    page_keys = jax.random.split(jax.random.fold_in(key, 11), PAGES)
    return jax.vmap(slot_row)(page_keys).astype(jnp.int32)


def draw_qkv_weight(key, part):
    normal_part = jax.random.normal(key, (3, DV, HEADS * HD), jnp.float32) * DV ** (-0.5)
    normal_part = jnp.clip(normal_part, -1.0, 1.0)
    return normal_part.astype(jnp.bfloat16)


def level_of(rng, dims, pieces, low, top_value):
    def one(dim, parts):
        steps = jax.random.uniform(jax.random.fold_in(jax.random.fold_in(rng, 6), dim), (parts,), jnp.float32, low / len(pieces), top_value / len(pieces))
        return jnp.repeat(jnp.exp(steps), dims[dim] // parts).reshape((-1,) + (1,) * (len(dims) - dim - 1))

    loudness = one(*pieces[0])
    for cut in pieces[1:]:
        loudness = loudness * one(*cut)
    return loudness


def normal_values(rng, dims, scale, bound, pieces=(), kind=jnp.bfloat16):
    loudness = level_of(rng, dims, pieces, -0.22, 0.18) if pieces else 1.0
    entries = jax.random.normal(rng, dims, jnp.float32) * scale * loudness
    return jnp.minimum(jnp.maximum(entries, -bound), bound).astype(kind)


def setup_inputs(seed: int = 0) -> dict:
    streams_of = jax.random.split(jax.random.key(seed), 8)
    return {
        "crops": normal_values(streams_of[0], (PAGES, SELMAX, CTOK, DV), 1.0, 6.0, ((0, 8), (1, 12), (2, 8))),
        "dout": normal_values(streams_of[1], (PAGES, SLOTS, CTOK, HEADS * HD), 0.1, 0.796875, ((0, 8), (1, 12), (3, 8))),
        "crop_count": draw_crop_count(jax.random.fold_in(streams_of[7], 71), 0),
        "crop_ids": jax.vmap(lambda own: jax.random.permutation(own, SELMAX))(jax.random.split(streams_of[3], PAGES)).reshape((PAGES, SELMAX)).astype(jnp.int32),
        "seq_slot": draw_seq_slot(jax.random.fold_in(streams_of[7], 71), 0),
        "norm_gain": jnp.clip(1.0 + 0.18 * jax.random.normal(streams_of[5], (DV,), jnp.float32), 0.099609375, 1.8984375).astype(jnp.bfloat16),
        "qkv_weight": draw_qkv_weight(jax.random.fold_in(streams_of[7], 71), 0),
    }


def crop_grads(inputs, cotangent, norm_gain, weight):
    crops_here, tok_count, head_cols = cotangent.shape
    head_count = head_cols // HD
    values = inputs.astype(jnp.float32)
    centred = values - lax.optimization_barrier(jnp.mean(values, axis=-1, keepdims=True))
    spread = lax.optimization_barrier(jnp.mean(centred * centred, axis=-1, keepdims=True))
    normed = (centred * lax.rsqrt(spread + 1e-05) * norm_gain.astype(jnp.float32)).astype(jnp.bfloat16)
    projected = jnp.einsum('etd,cdw->cetw', normed.astype(jnp.float32), weight.astype(jnp.float32)).astype(jnp.bfloat16)
    heads_view = projected.reshape(3, crops_here, tok_count, head_count, HD)
    queries = heads_view[0].astype(jnp.float32)
    key_rows = heads_view[1].astype(jnp.float32)
    value_rows = heads_view[2].astype(jnp.float32)
    score_scale = HD ** (-0.5)
    scores = jnp.einsum('eqhd,ekhd->ehqk', queries, key_rows) * score_scale
    attention = jax.nn.softmax(scores, axis=-1)
    attention_low = attention.astype(jnp.bfloat16).astype(jnp.float32)
    upstream = cotangent.reshape(crops_here, tok_count, head_count, HD).astype(jnp.float32)
    grad_values = jnp.einsum('ehqk,eqhd->ekhd', attention_low, upstream).astype(jnp.bfloat16)
    grad_attention = jnp.einsum('eqhd,ekhd->ehqk', upstream, value_rows)
    grad_scores = attention * (grad_attention - lax.optimization_barrier(jnp.sum(attention * grad_attention, axis=-1, keepdims=True)))
    scaled = (grad_scores * score_scale).astype(jnp.bfloat16).astype(jnp.float32)
    grad_queries = jnp.einsum('ehqk,ekhd->eqhd', scaled, key_rows).astype(jnp.bfloat16)
    grad_keys = jnp.einsum('ehqk,eqhd->ekhd', scaled, queries).astype(jnp.bfloat16)
    stacked = jnp.stack([grad_queries, grad_keys, grad_values]).reshape(3, crops_here, tok_count, head_cols)
    return jnp.einsum('etd,cetw->cdw', normed.astype(jnp.float32), stacked.astype(jnp.float32))

def reference(crops, dout, crop_count, crop_ids, seq_slot, norm_gain, qkv_weight):
    most_crops = crop_ids.shape[1]
    page_total = crops.shape[0]
    head_cols = dout.shape[3]

    def accumulate(running, position):
        page_no = (position // most_crops).astype(jnp.int32)
        rank_no = (position % most_crops).astype(jnp.int32)
        is_live = rank_no < crop_count[page_no]
        candidate = crop_ids[page_no, rank_no].astype(jnp.int32)
        slot_no = seq_slot[page_no, rank_no].astype(jnp.int32)
        inputs = crops[page_no, candidate][None]
        cotangent = dout[page_no, slot_no][None]
        local_grad = crop_grads(inputs, cotangent, norm_gain, qkv_weight)
        return (running + jnp.where(is_live, local_grad, jnp.zeros_like(local_grad)), None)
    start_grad = jnp.zeros((3, crops.shape[3], head_cols), jnp.float32)
    running, _ = lax.scan(accumulate, start_grad, jnp.arange(page_total * most_crops, dtype=jnp.int32))
    return running.reshape(3 * crops.shape[3], head_cols)
```

```python
import jax
import jax.numpy as jnp
from jax import lax
from jax.sharding import Mesh, PartitionSpec as P

HD = 64
GRP_OUTER = 4
GRP_INNER = 2


def layer_norm(inputs, norm_gain):
    values = inputs.astype(jnp.float32)
    centred = values - jnp.mean(values, axis=-1, keepdims=True)
    spread = jnp.mean(centred * centred, axis=-1, keepdims=True)
    return (centred * lax.rsqrt(spread + 1e-05) * norm_gain.astype(jnp.float32)).astype(
        jnp.bfloat16
    )


def weight_partials(normed, cotangent, weight):
    tok_count, head_cols = cotangent.shape
    head_count = head_cols // HD
    projected = jnp.einsum(
        "td,cdw->ctw", normed, weight, preferred_element_type=jnp.float32
    ).astype(jnp.bfloat16)
    heads_view = projected.reshape(3, tok_count, head_count, HD)
    queries, key_rows, value_rows = heads_view[0], heads_view[1], heads_view[2]
    score_scale = HD ** (-0.5)
    scores = (
        jnp.einsum("qhd,khd->hqk", queries, key_rows, preferred_element_type=jnp.float32)
        * score_scale
    )
    attention = jax.nn.softmax(scores, axis=-1)
    attention_low = attention.astype(jnp.bfloat16)
    upstream = cotangent.reshape(tok_count, head_count, HD)
    grad_values = jnp.einsum(
        "hqk,qhd->khd", attention_low, upstream, preferred_element_type=jnp.float32
    ).astype(jnp.bfloat16)
    grad_attention = jnp.einsum(
        "qhd,khd->hqk", upstream, value_rows, preferred_element_type=jnp.float32
    )
    grad_scores = attention * (
        grad_attention - jnp.sum(attention * grad_attention, axis=-1, keepdims=True)
    )
    scaled = (grad_scores * score_scale).astype(jnp.bfloat16)
    grad_queries = jnp.einsum(
        "hqk,khd->qhd", scaled, key_rows, preferred_element_type=jnp.float32
    ).astype(jnp.bfloat16)
    grad_keys = jnp.einsum(
        "hqk,qhd->khd", scaled, queries, preferred_element_type=jnp.float32
    ).astype(jnp.bfloat16)
    stacked = jnp.stack([grad_queries, grad_keys, grad_values]).reshape(3, tok_count, head_cols)
    return jnp.einsum("td,ctw->cdw", normed, stacked, preferred_element_type=jnp.float32)


def slot_selector(crop_count, crop_ids, seq_slot):
    most = crop_ids.shape[0]
    numbers = jnp.arange(most, dtype=jnp.int32)
    live = numbers < crop_count
    from_candidate = (crop_ids[None, :] == numbers[:, None]) & live[None, :]
    to_slot = seq_slot[:, None] == numbers[None, :]
    return jnp.dot(from_candidate.astype(jnp.float32), to_slot.astype(jnp.float32))


def make_body(seq_size):
    def body(crops, dout, crop_count, crop_ids, seq_slot, norm_gain, qkv_weight):
        tok_local, width = crops.shape[2:]
        tok_count, head_cols = dout.shape[2:]
        tp_size = tok_count // tok_local
        chunk = tok_count // seq_size

        pieces = lax.all_to_all(
            dout[0, 0].reshape(seq_size, chunk, head_cols), "z", 0, 0, tiled=True
        )
        selector = slot_selector(crop_count[0], crop_ids[0], seq_slot[0]).astype(jnp.bfloat16)
        routed = jnp.einsum(
            "cs,sjw->cjw", selector, pieces, preferred_element_type=jnp.float32
        ).astype(jnp.bfloat16)
        cotangent = lax.all_to_all(routed, "z", 0, 0, tiled=True).reshape(tok_count, head_cols)

        local = layer_norm(crops[0, 0], norm_gain)
        normed = lax.all_to_all(
            jnp.broadcast_to(local[None], (tp_size, tok_local, width)), ("yl", "x"), 0, 0, tiled=True
        ).reshape(tok_count, width)

        partial = weight_partials(normed, cotangent, qkv_weight)

        rows = 3 * width // (GRP_OUTER * GRP_INNER * seq_size)
        core = lax.axis_index("core")
        by_core = partial.reshape(GRP_OUTER, GRP_INNER, seq_size * rows, head_cols)
        theirs = lax.dynamic_index_in_dim(by_core, 1 - core, 1, keepdims=False)
        mine = lax.dynamic_index_in_dim(by_core, core, 1, keepdims=False)
        received = lax.ppermute(theirs.astype(jnp.bfloat16), "core", [(0, 1), (1, 0)])
        total = mine + received.astype(jnp.float32)
        parts = lax.all_to_all(total.astype(jnp.bfloat16), "yh", 0, 0, tiled=True)
        total = jnp.sum(parts.astype(jnp.float32), axis=0)
        parts = lax.all_to_all(
            total.astype(jnp.bfloat16).reshape(seq_size, rows, head_cols), "z", 0, 0, tiled=True
        )
        return jnp.sum(parts.astype(jnp.float32), axis=0)

    return body


def solution(mesh):
    seq_size = mesh.shape["seq"]
    tp_inner = mesh.shape["tp"] // 2
    fine = Mesh(
        mesh.devices.reshape(GRP_OUTER, GRP_INNER, 2, tp_inner, seq_size),
        ("yh", "core", "yl", "x", "z"),
    )
    grp, tp = ("yh", "core"), ("yl", "x")
    in_specs = (
        P(grp, "z", tp, None),
        P(grp, "z", None, tp),
        P(grp),
        P(grp, None),
        P(grp, None),
        P(),
        P(None, None, tp),
    )
    out_specs = P((*grp, "z"), tp)
    return jax.shard_map(
        make_body(seq_size), mesh=fine, in_specs=in_specs, out_specs=out_specs, check_vma=False
    )
```

```python
import jax
import jax.numpy as jnp
from jax import lax
from jax.experimental import pallas as pl
from jax.experimental.pallas import tpu as pltpu
from jax.sharding import Mesh, PartitionSpec as P


HD = 64
GRP_OUTER = 4
GRP_INNER = 2
TP_OUTER = 2

NN = (((1,), (0,)), ((), ()))
NT = (((1,), (1,)), ((), ()))
VMEM = pl.BlockSpec(memory_space=pltpu.VMEM)
SMEM = pl.BlockSpec(memory_space=pltpu.SMEM)
ANY = pl.BlockSpec(memory_space=pl.ANY)


def dot(a, b, dims=NN):
    return lax.dot_general(a, b, dims, preferred_element_type=jnp.float32)


def norm_kernel(inputs_ref, gain_ref, out_ref):
    values = inputs_ref[...].astype(jnp.float32)
    centred = values - jnp.mean(values, axis=-1, keepdims=True)
    spread = jnp.mean(centred * centred, axis=-1, keepdims=True)
    normed = centred * lax.rsqrt(spread + 1e-05) * gain_ref[...].astype(jnp.float32)
    out_ref[...] = normed.astype(jnp.bfloat16)


def layer_norm(inputs, gain):
    return pl.pallas_call(
        norm_kernel,
        out_shape=jax.ShapeDtypeStruct(inputs.shape, jnp.bfloat16),
        in_specs=[VMEM, VMEM],
        out_specs=VMEM,
        name="norm",
    )(inputs, gain)


def route_kernel(count_ref, ids_ref, slot_ref, pieces_hbm, out_ref, pieces_ref, sem):
    copy = pltpu.make_async_copy(pieces_hbm, pieces_ref, sem)
    copy.start()
    out_ref[...] = jnp.zeros(out_ref.shape, out_ref.dtype)
    copy.wait()
    for rank in range(out_ref.shape[0]):

        @pl.when(rank < count_ref[0])
        def _():
            out_ref[ids_ref[0, rank]] = pieces_ref[slot_ref[0, rank]]


def by_candidate(count, ids, slots, pieces):
    return pl.pallas_call(
        route_kernel,
        out_shape=jax.ShapeDtypeStruct(pieces.shape, pieces.dtype),
        in_specs=[SMEM, SMEM, SMEM, ANY],
        out_specs=VMEM,
        scratch_shapes=[pltpu.VMEM(pieces.shape, pieces.dtype), pltpu.SemaphoreType.DMA(())],
        name="route",
    )(count, ids, slots, pieces)


def grads_kernel(place_ref, *refs):
    *block_refs, weight_ref, cotangent_hbm = refs[:-7]
    theirs_ref, mine_ref, sums_ref, blocks_ref, cotangent_ref, block_sems, cotangent_sem = refs[-7:]
    low = jnp.bfloat16
    copies = [
        pltpu.make_async_copy(ref, blocks_ref.at[i], block_sems.at[i])
        for i, ref in enumerate(block_refs)
    ]
    copies.append(pltpu.make_async_copy(cotangent_hbm, cotangent_ref, cotangent_sem))
    for copy in copies:
        copy.start()
    for copy in copies:
        copy.wait()
    normed = jnp.concatenate([blocks_ref[i] for i in range(len(block_refs))], 0)
    tok_count, width = normed.shape
    head_cols = cotangent_ref.shape[1]
    queries = dot(normed, weight_ref[0]).astype(low)
    key_rows = dot(normed, weight_ref[1]).astype(low)
    value_rows = dot(normed, weight_ref[2]).astype(low)
    first = place_ref[1] * blocks_ref.shape[1]
    turn = jnp.where(first == 0, 0, tok_count - first)
    upstream = pltpu.roll(cotangent_ref[...].astype(jnp.float32), turn, 0).astype(low)
    head_of = lax.broadcasted_iota(jnp.int32, (tok_count, head_cols), 1) // HD
    zero = jnp.zeros((), low)
    score_scale = HD ** (-0.5)
    keys_t = key_rows.T
    grad_values, grad_keys, grad_queries = [], [], []
    for head in range(head_cols // HD):
        q = jnp.where(head_of == head, queries, zero)
        g = jnp.where(head_of == head, upstream, zero)
        scores = dot(key_rows, q, NT) * score_scale
        weights = jnp.exp(scores - jnp.max(scores, axis=0, keepdims=True))
        attention = weights / jnp.sum(weights, axis=0, keepdims=True)
        grad_attention = dot(value_rows, g, NT)
        mean = jnp.sum(attention * grad_attention, axis=0, keepdims=True)
        scaled = (attention * (grad_attention - mean) * score_scale).astype(low)
        grad_values.append(dot(attention.astype(low), g))
        grad_keys.append(dot(scaled, q))
        grad_queries.append(dot(keys_t[head * HD : (head + 1) * HD], scaled))
    normed_t = normed.T
    joined = (
        jnp.concatenate(grad_queries, 0).astype(low).T,
        sum(grad_keys).astype(low),
        sum(grad_values).astype(low),
    )
    for c, grad in enumerate(joined):
        sums_ref[pl.ds(c * width, width), :] = dot(normed_t, grad)
    core = place_ref[0]
    seq_size, outer_rows = theirs_ref.shape[:2]
    rows = outer_rows // GRP_OUTER
    for outer in range(GRP_OUTER):
        own = (outer * GRP_INNER + core) * seq_size * rows
        other = (outer * GRP_INNER + 1 - core) * seq_size * rows
        for s in range(seq_size):
            to = pl.ds(outer * rows, rows)
            mine_ref[s, to] = sums_ref[pl.ds(pl.multiple_of(own + s * rows, rows), rows), :]
            theirs_ref[s, to] = sums_ref[
                pl.ds(pl.multiple_of(other + s * rows, rows), rows), :
            ].astype(low)


def weight_partials(place, normed, weight, cotangent, seq_size):
    width, head_cols = weight.shape[1:]
    half = (seq_size, 3 * width // (GRP_INNER * seq_size), head_cols)
    return pl.pallas_call(
        grads_kernel,
        out_shape=(
            jax.ShapeDtypeStruct(half, jnp.bfloat16),
            jax.ShapeDtypeStruct(half, jnp.float32),
        ),
        in_specs=[SMEM, *[ANY] * len(normed), VMEM, ANY],
        out_specs=(VMEM, VMEM),
        scratch_shapes=[
            pltpu.VMEM((3 * width, head_cols), jnp.float32),
            pltpu.VMEM((len(normed), *normed[0].shape), jnp.bfloat16),
            pltpu.VMEM(cotangent.shape, jnp.bfloat16),
            pltpu.SemaphoreType.DMA((len(normed),)),
            pltpu.SemaphoreType.DMA(()),
        ],
        name="grads",
    )(place, *normed, weight, cotangent)


def make_body(seq_size):
    def body(crops, dout, crop_count, crop_ids, seq_slot, norm_gain, qkv_weight):
        return step(crops, dout, crop_count, crop_ids, seq_slot, norm_gain, qkv_weight)

    def step(crops, dout, crop_count, crop_ids, seq_slot, norm_gain, qkv_weight):
        tok_local, _ = crops.shape[2:]
        tok_count, head_cols = dout.shape[2:]
        tp_size = tok_count // tok_local
        chunk = tok_count // seq_size

        pieces = lax.all_to_all(
            dout[0, 0].reshape(seq_size, chunk, head_cols), "z", 0, 0, tiled=True
        )
        routed = by_candidate(crop_count, crop_ids, seq_slot, pieces)
        cotangent = lax.all_to_all(routed, "z", 0, 0, tiled=True)
        cotangent = cotangent.reshape(tok_count, head_cols)

        local = layer_norm(crops[0, 0], norm_gain[None])
        tp = ("yl", "x")
        normed = [local]
        for d in range(1, tp_size):
            pairs = [(i, (i - d) % tp_size) for i in range(tp_size)]
            normed.append(lax.ppermute(local, tp, pairs))

        place = jnp.stack([lax.axis_index("core"), lax.axis_index(tp)])
        theirs, mine = weight_partials(place, normed, qkv_weight, cotangent, seq_size)

        received = lax.ppermute(theirs, "core", [(0, 1), (1, 0)])
        total = mine + received.astype(jnp.float32)
        parts = lax.all_to_all(total.astype(jnp.bfloat16), "z", 0, 0, tiled=True)
        total = jnp.sum(parts.astype(jnp.float32), axis=0)
        parts = lax.all_to_all(
            total.astype(jnp.bfloat16).reshape(GRP_OUTER, -1, head_cols), "yh", 0, 0, tiled=True
        )
        return jnp.sum(parts.astype(jnp.float32), axis=0)

    return body


def solution(mesh):
    seq_size = mesh.shape["seq"]
    tp_inner = mesh.shape["tp"] // TP_OUTER
    fine = Mesh(
        mesh.devices.reshape(GRP_OUTER, GRP_INNER, TP_OUTER, tp_inner, seq_size),
        ("yh", "core", "yl", "x", "z"),
    )
    grp, tp = ("yh", "core"), ("yl", "x")
    in_specs = (
        P(grp, "z", tp, None),
        P(grp, "z", None, tp),
        P(grp),
        P(grp, None),
        P(grp, None),
        P(),
        P(None, None, tp),
    )
    out_specs = P((*grp, "z"), tp)
    return jax.shard_map(
        make_body(seq_size), mesh=fine, in_specs=in_specs, out_specs=out_specs, check_vma=False
    )
```

```python
import jax
import jax.numpy as jnp
from jax import lax
from jax.experimental import pallas as pl
from jax.experimental.pallas import tpu as pltpu
from jax.sharding import Mesh, PartitionSpec as P


HD = 64
GRP_OUTER = 4
GRP_INNER = 2
TP_OUTER = 2
KERNEL_VMEM = 28 << 20

NN = (((1,), (0,)), ((), ()))
NT = (((1,), (1,)), ((), ()))
VMEM = pl.BlockSpec(memory_space=pltpu.VMEM)
SMEM = pl.BlockSpec(memory_space=pltpu.SMEM)


def near(value):
    return pltpu.with_memory_space_constraint(value, pltpu.VMEM)


def dot(a, b, dims=NN):
    return lax.dot_general(a, b, dims, preferred_element_type=jnp.float32)


def norm_kernel(inputs_ref, gain_ref, out_ref):
    values = inputs_ref[...].astype(jnp.float32)
    centred = values - jnp.mean(values, axis=-1, keepdims=True)
    spread = jnp.mean(centred * centred, axis=-1, keepdims=True)
    normed = centred * lax.rsqrt(spread + 1e-05) * gain_ref[...].astype(jnp.float32)
    out_ref[...] = normed.astype(jnp.bfloat16)


def layer_norm(inputs, gain):
    return pl.pallas_call(
        norm_kernel,
        out_shape=jax.ShapeDtypeStruct(inputs.shape, jnp.bfloat16),
        in_specs=[VMEM, VMEM],
        out_specs=VMEM,
        name="norm",
    )(inputs, gain)


def route_kernel(count_ref, ids_ref, slot_ref, pieces_ref, out_ref):
    out_ref[...] = jnp.zeros(out_ref.shape, out_ref.dtype)
    for rank in range(out_ref.shape[0]):

        @pl.when(rank < count_ref[0])
        def _():
            out_ref[ids_ref[0, rank]] = pieces_ref[slot_ref[0, rank]]


def by_candidate(count, ids, slots, pieces):
    return pl.pallas_call(
        route_kernel,
        out_shape=pltpu.VMEM(pieces.shape, pieces.dtype),
        in_specs=[SMEM, SMEM, SMEM, VMEM],
        out_specs=VMEM,
        name="route",
    )(count, ids, slots, pieces)


def grads_kernel(place_ref, *refs):
    *block_refs, weight_ref, cotangent_ref, theirs_ref, mine_ref, sums_ref = refs
    low = jnp.bfloat16
    both = block_refs[0].shape[0]
    part = both // TP_OUTER
    blocks = [ref[...] for ref in block_refs]
    normed = jnp.concatenate(
        [block[i * part : (i + 1) * part] for i in range(TP_OUTER) for block in blocks], 0
    )
    tok_count, width = normed.shape
    head_cols = cotangent_ref.shape[1]
    queries = dot(normed, weight_ref[0]).astype(low)
    key_rows = dot(normed, weight_ref[1]).astype(low)
    value_rows = dot(normed, weight_ref[2]).astype(low)
    half = tok_count // TP_OUTER
    first = place_ref[1] * part
    turn = jnp.where(first == 0, 0, half - first)
    upstream = cotangent_ref[...].astype(jnp.float32)
    upstream = jnp.concatenate(
        [pltpu.roll(upstream[i * half : (i + 1) * half], turn, 0) for i in range(TP_OUTER)], 0
    ).astype(low)
    head_of = lax.broadcasted_iota(jnp.int32, (tok_count, head_cols), 1) // HD
    zero = jnp.zeros((), low)
    score_scale = HD ** (-0.5)
    keys_t = key_rows.T
    grad_values, grad_keys, grad_queries = [], [], []
    for head in range(head_cols // HD):
        q = jnp.where(head_of == head, queries, zero)
        g = jnp.where(head_of == head, upstream, zero)
        scores = dot(key_rows, q, NT) * score_scale
        weights = jnp.exp(scores - jnp.max(scores, axis=0, keepdims=True))
        attention = weights / jnp.sum(weights, axis=0, keepdims=True)
        grad_attention = dot(value_rows, g, NT)
        mean = jnp.sum(attention * grad_attention, axis=0, keepdims=True)
        scaled = (attention * (grad_attention - mean) * score_scale).astype(low)
        grad_values.append(dot(attention.astype(low), g))
        grad_keys.append(dot(scaled, q))
        grad_queries.append(dot(keys_t[head * HD : (head + 1) * HD], scaled))
    normed_t = normed.T
    joined = (
        jnp.concatenate(grad_queries, 0).astype(low).T,
        sum(grad_keys).astype(low),
        sum(grad_values).astype(low),
    )
    for c, grad in enumerate(joined):
        sums_ref[pl.ds(c * width, width), :] = dot(normed_t, grad)
    core = place_ref[0]
    rows = theirs_ref.shape[1]
    for outer in range(GRP_OUTER):
        own = pl.multiple_of((outer * GRP_INNER + core) * rows, rows)
        other = pl.multiple_of((outer * GRP_INNER + 1 - core) * rows, rows)
        mine_ref[outer] = sums_ref[pl.ds(own, rows), :]
        theirs_ref[outer] = sums_ref[pl.ds(other, rows), :].astype(low)


def weight_partials(place, normed, weight, cotangent):
    width, head_cols = weight.shape[1:]
    half = (GRP_OUTER, 3 * width // (GRP_OUTER * GRP_INNER), head_cols)
    return pl.pallas_call(
        grads_kernel,
        out_shape=(
            pltpu.VMEM(half, jnp.bfloat16),
            pltpu.VMEM(half, jnp.float32),
        ),
        in_specs=[SMEM, *[VMEM] * len(normed), VMEM, VMEM],
        out_specs=(VMEM, VMEM),
        scratch_shapes=[pltpu.VMEM((3 * width, head_cols), jnp.float32)],
        compiler_params=pltpu.CompilerParams(vmem_limit_bytes=KERNEL_VMEM),
        name="grads",
    )(place, *normed, weight, cotangent)


def make_body(seq_size):
    def body(crops, dout, crop_count, crop_ids, seq_slot, norm_gain, qkv_weight):
        return step(crops, dout, crop_count, crop_ids, seq_slot, norm_gain, qkv_weight)

    def step(crops, dout, crop_count, crop_ids, seq_slot, norm_gain, qkv_weight):
        tok_local, _ = crops.shape[2:]
        tok_count, head_cols = dout.shape[2:]
        tp_inner = tok_count // tok_local // TP_OUTER
        chunk = tok_count // seq_size

        pieces = lax.all_to_all(
            dout[0, 0].reshape(seq_size, chunk, head_cols), "z", 0, 0, tiled=True
        )
        routed = by_candidate(crop_count, crop_ids, seq_slot, near(pieces))
        cotangent = lax.all_to_all(routed, "z", 0, 0, tiled=True)
        cotangent = cotangent.reshape(tok_count, head_cols)

        local = layer_norm(crops[0, 0], norm_gain[None])
        both = lax.all_gather(local, "yl", axis=0, tiled=True)
        normed = [near(both)]
        for d in range(1, tp_inner):
            pairs = [(i, (i - d) % tp_inner) for i in range(tp_inner)]
            normed.append(near(lax.ppermute(both, "x", pairs)))

        place = jnp.stack([lax.axis_index("core"), lax.axis_index("x")])
        theirs, mine = weight_partials(place, normed, near(qkv_weight), near(cotangent))

        received = lax.ppermute(theirs, "core", [(0, 1), (1, 0)])
        total = (mine + received.astype(jnp.float32)).astype(jnp.bfloat16)
        total = total.reshape(GRP_OUTER * seq_size, -1, head_cols)
        parts = lax.all_to_all(total, ("yh", "z"), 0, 0, tiled=True)
        return jnp.sum(parts.astype(jnp.float32), axis=0)

    return body


def solution(mesh):
    seq_size = mesh.shape["seq"]
    tp_inner = mesh.shape["tp"] // TP_OUTER
    fine = Mesh(
        mesh.devices.reshape(GRP_OUTER, GRP_INNER, TP_OUTER, tp_inner, seq_size),
        ("yh", "core", "yl", "x", "z"),
    )
    grp, tp = ("yh", "core"), ("yl", "x")
    in_specs = (
        P(grp, "z", tp, None),
        P(grp, "z", None, tp),
        P(grp),
        P(grp, None),
        P(grp, None),
        P(),
        P(None, None, tp),
    )
    out_specs = P((*grp, "z"), tp)
    return jax.shard_map(
        make_body(seq_size), mesh=fine, in_specs=in_specs, out_specs=out_specs, check_vma=False
    )
```

```python
import functools

import jax
import jax.numpy as jnp
from jax import lax
from jax.experimental import pallas as pl
from jax.experimental.pallas import tpu as pltpu
from jax.sharding import Mesh, PartitionSpec as P


HD = 64
GRP_OUTER = 4
GRP_INNER = 2
TP_OUTER = 2
KERNEL_VMEM = 24 << 20

NN = (((1,), (0,)), ((), ()))
NT = (((1,), (1,)), ((), ()))
VMEM = pl.BlockSpec(memory_space=pltpu.VMEM)
SMEM = pl.BlockSpec(memory_space=pltpu.SMEM)


def near(value):
    return pltpu.with_memory_space_constraint(value, pltpu.VMEM)


def dot(a, b, dims=NN):
    return lax.dot_general(a, b, dims, preferred_element_type=jnp.float32)


def norm_kernel(inputs_ref, gain_ref, out_ref):
    values = inputs_ref[...].astype(jnp.float32)
    centred = values - jnp.mean(values, axis=-1, keepdims=True)
    spread = jnp.mean(centred * centred, axis=-1, keepdims=True)
    normed = centred * lax.rsqrt(spread + 1e-05) * gain_ref[...][None].astype(jnp.float32)
    out_ref[...] = normed.astype(jnp.bfloat16)


def layer_norm(inputs, gain):
    return pl.pallas_call(
        norm_kernel,
        out_shape=jax.ShapeDtypeStruct(inputs.shape, jnp.bfloat16),
        in_specs=[VMEM, VMEM],
        out_specs=VMEM,
        name="norm",
    )(inputs, gain)


def route_kernel(count_ref, ids_ref, slot_ref, pieces_ref, out_ref):
    out_ref[...] = jnp.zeros(out_ref.shape, out_ref.dtype)
    for rank in range(out_ref.shape[0]):

        @pl.when(rank < count_ref[0])
        def _():
            out_ref[ids_ref[0, rank]] = pieces_ref[slot_ref[0, rank]]


def by_candidate(count, ids, slots, pieces):
    return pl.pallas_call(
        route_kernel,
        out_shape=pltpu.VMEM(pieces.shape, pieces.dtype),
        in_specs=[SMEM, SMEM, SMEM, VMEM],
        out_specs=VMEM,
        name="route",
    )(count, ids, slots, pieces)


def head_mask(shape, head):
    return lax.broadcasted_iota(jnp.int32, shape, 1) // HD == head


def project_kernel(*refs):
    *block_refs, weight_ref, projected_ref, normed_t_ref = refs
    low = jnp.bfloat16
    part = block_refs[0].shape[0] // TP_OUTER
    blocks = [ref[...] for ref in block_refs]
    normed = jnp.concatenate(
        [block[i * part : (i + 1) * part] for i in range(TP_OUTER) for block in blocks], 0
    )
    for c in range(3):
        projected_ref[c] = dot(normed, weight_ref[c]).astype(low)
    normed_t_ref[...] = normed.T


def project(normed, weight):
    width, head_cols = weight.shape[1:]
    tok_count = sum(block.shape[0] for block in normed)
    return pl.pallas_call(
        project_kernel,
        out_shape=(
            pltpu.VMEM((3, tok_count, head_cols), jnp.bfloat16),
            pltpu.VMEM((width, tok_count), jnp.bfloat16),
        ),
        in_specs=[VMEM] * (len(normed) + 1),
        out_specs=(VMEM, VMEM),
        compiler_params=pltpu.CompilerParams(vmem_limit_bytes=KERNEL_VMEM),
        name="project",
    )(*normed, weight)


def grads_kernel(
    place_ref,
    projected_ref,
    normed_t_ref,
    cotangent_ref,
    theirs_ref,
    mine_ref,
    sums_ref,
    *,
    part,
):
    low = jnp.bfloat16
    tok_count, head_cols = cotangent_ref.shape
    width = normed_t_ref.shape[0]
    queries, key_rows, value_rows = projected_ref[0], projected_ref[1], projected_ref[2]
    half = tok_count // TP_OUTER
    first = place_ref[1] * part
    turn = jnp.where(first == 0, 0, half - first)
    upstream = cotangent_ref[...].astype(jnp.float32)
    upstream = jnp.concatenate(
        [pltpu.roll(upstream[i * half : (i + 1) * half], turn, 0) for i in range(TP_OUTER)], 0
    ).astype(low)
    zero = jnp.zeros((), low)
    score_scale = HD ** (-0.5)
    keys_t = key_rows.T
    grad_values, grad_keys, grad_queries = [], [], []
    for head in range(head_cols // HD):
        own = head_mask(queries.shape, head)
        q = jnp.where(own, queries, zero)
        g = jnp.where(own, upstream, zero)
        scores = dot(key_rows, q, NT) * score_scale
        weights = jnp.exp(scores - jnp.max(scores, axis=0, keepdims=True))
        attention = weights / jnp.sum(weights, axis=0, keepdims=True)
        grad_attention = dot(value_rows, g, NT)
        mean = jnp.sum(attention * grad_attention, axis=0, keepdims=True)
        scaled = (attention * (grad_attention - mean) * score_scale).astype(low)
        grad_values.append(dot(attention.astype(low), g))
        grad_keys.append(dot(scaled, q))
        grad_queries.append(dot(keys_t[head * HD : (head + 1) * HD], scaled))
    normed_t = normed_t_ref[...]
    joined = (
        jnp.concatenate(grad_queries, 0).astype(low).T,
        sum(grad_keys).astype(low),
        sum(grad_values).astype(low),
    )
    for c, grad in enumerate(joined):
        sums_ref[pl.ds(c * width, width), :] = dot(normed_t, grad)
    core = place_ref[0]
    rows = theirs_ref.shape[1]
    for outer in range(GRP_OUTER):
        own = pl.multiple_of((outer * GRP_INNER + core) * rows, rows)
        other = pl.multiple_of((outer * GRP_INNER + 1 - core) * rows, rows)
        mine_ref[outer] = sums_ref[pl.ds(own, rows), :]
        theirs_ref[outer] = sums_ref[pl.ds(other, rows), :].astype(low)


def weight_partials(place, projected, normed_t, cotangent, part):
    width, head_cols = normed_t.shape[0], cotangent.shape[1]
    half = (GRP_OUTER, 3 * width // (GRP_OUTER * GRP_INNER), head_cols)
    return pl.pallas_call(
        functools.partial(grads_kernel, part=part),
        out_shape=(
            pltpu.VMEM(half, jnp.bfloat16),
            pltpu.VMEM(half, jnp.float32),
        ),
        in_specs=[SMEM, VMEM, VMEM, VMEM],
        out_specs=(VMEM, VMEM),
        scratch_shapes=[pltpu.VMEM((3 * width, head_cols), jnp.float32)],
        compiler_params=pltpu.CompilerParams(vmem_limit_bytes=KERNEL_VMEM),
        name="grads",
    )(place, projected, normed_t, cotangent)


def make_body(seq_size):
    def body(crops, dout, crop_count, crop_ids, seq_slot, norm_gain, qkv_weight):
        return step(crops, dout, crop_count, crop_ids, seq_slot, norm_gain, qkv_weight)

    def step(crops, dout, crop_count, crop_ids, seq_slot, norm_gain, qkv_weight):
        tok_local, _ = crops.shape[2:]
        tok_count, head_cols = dout.shape[2:]
        tp_inner = tok_count // tok_local // TP_OUTER
        chunk = tok_count // seq_size

        pieces = lax.all_to_all(
            dout[0, 0].reshape(seq_size, chunk, head_cols), "z", 0, 0, tiled=True
        )
        routed = by_candidate(crop_count, crop_ids, seq_slot, near(pieces))
        cotangent = lax.all_to_all(routed, "z", 0, 0, tiled=True)
        cotangent = cotangent.reshape(tok_count, head_cols)

        local = layer_norm(crops[0, 0], norm_gain)
        both = lax.all_gather(local, "yl", axis=0, tiled=True)
        normed = [near(both)]
        for d in range(1, tp_inner):
            pairs = [(i, (i - d) % tp_inner) for i in range(tp_inner)]
            normed.append(near(lax.ppermute(both, "x", pairs)))

        kept = project(normed, qkv_weight)
        place = jnp.stack([lax.axis_index("core"), lax.axis_index("x")])
        theirs, mine = weight_partials(
            place, *[near(value) for value in kept], near(cotangent), tok_local
        )

        received = lax.ppermute(theirs, "core", [(0, 1), (1, 0)])
        total = (mine + received.astype(jnp.float32)).astype(jnp.bfloat16)
        total = total.reshape(GRP_OUTER * seq_size, -1, head_cols)
        parts = lax.all_to_all(total, ("yh", "z"), 0, 0, tiled=True)
        return jnp.sum(parts.astype(jnp.float32), axis=0)

    return body


def solution(mesh):
    seq_size = mesh.shape["seq"]
    tp_inner = mesh.shape["tp"] // TP_OUTER
    fine = Mesh(
        mesh.devices.reshape(GRP_OUTER, GRP_INNER, TP_OUTER, tp_inner, seq_size),
        ("yh", "core", "yl", "x", "z"),
    )
    grp, tp = ("yh", "core"), ("yl", "x")
    in_specs = (
        P(grp, "z", tp, None),
        P(grp, "z", None, tp),
        P(grp),
        P(grp, None),
        P(grp, None),
        P(),
        P(None, None, tp),
    )
    out_specs = P((*grp, "z"), tp)
    return jax.shard_map(
        make_body(seq_size), mesh=fine, in_specs=in_specs, out_specs=out_specs, check_vma=False
    )
```

```python
import functools

import jax
import jax.numpy as jnp
from jax import lax
from jax.experimental import pallas as pl
from jax.experimental.pallas import tpu as pltpu
from jax.sharding import Mesh, PartitionSpec as P


HD = 64
GRP_OUTER = 4
GRP_INNER = 2
TP_OUTER = 2
KERNEL_VMEM = 24 << 20

NN = (((1,), (0,)), ((), ()))
NT = (((1,), (1,)), ((), ()))
VMEM = pl.BlockSpec(memory_space=pltpu.VMEM)
SMEM = pl.BlockSpec(memory_space=pltpu.SMEM)


def near(value):
    return pltpu.with_memory_space_constraint(value, pltpu.VMEM)


def dot(a, b, dims=NN):
    return lax.dot_general(a, b, dims, preferred_element_type=jnp.float32)


def norm_kernel(inputs_ref, gain_ref, out_ref):
    values = inputs_ref[...].astype(jnp.float32)
    centred = values - jnp.mean(values, axis=-1, keepdims=True)
    spread = jnp.mean(centred * centred, axis=-1, keepdims=True)
    normed = centred * lax.rsqrt(spread + 1e-05) * gain_ref[...][None].astype(jnp.float32)
    out_ref[...] = normed.astype(jnp.bfloat16)


def layer_norm(inputs, gain):
    return pl.pallas_call(
        norm_kernel,
        out_shape=jax.ShapeDtypeStruct(inputs.shape, jnp.bfloat16),
        in_specs=[VMEM, VMEM],
        out_specs=VMEM,
        name="norm",
    )(inputs, gain)


def route_kernel(count_ref, ids_ref, slot_ref, pieces_ref, out_ref):
    out_ref[...] = jnp.zeros(out_ref.shape, out_ref.dtype)
    for rank in range(out_ref.shape[0]):

        @pl.when(rank < count_ref[0])
        def _():
            out_ref[ids_ref[0, rank]] = pieces_ref[slot_ref[0, rank]]


def by_candidate(count, ids, slots, pieces):
    return pl.pallas_call(
        route_kernel,
        out_shape=pltpu.VMEM(pieces.shape, pieces.dtype),
        in_specs=[SMEM, SMEM, SMEM, VMEM],
        out_specs=VMEM,
        name="route",
    )(count, ids, slots, pieces)


def head_mask(shape, head):
    return lax.broadcasted_iota(jnp.int32, shape, 1) // HD == head


def project_kernel(*refs):
    *block_refs, weight_ref, projected_ref, normed_t_ref = refs
    low = jnp.bfloat16
    part = block_refs[0].shape[0] // TP_OUTER
    blocks = [ref[...] for ref in block_refs]
    normed = jnp.concatenate(
        [block[i * part : (i + 1) * part] for i in range(TP_OUTER) for block in blocks], 0
    )
    for c in range(3):
        projected_ref[c] = dot(normed, weight_ref[c]).astype(low)
    normed_t_ref[...] = normed.T


def project(normed, weight):
    width, head_cols = weight.shape[1:]
    tok_count = sum(block.shape[0] for block in normed)
    return pl.pallas_call(
        project_kernel,
        out_shape=(
            pltpu.VMEM((3, tok_count, head_cols), jnp.bfloat16),
            pltpu.VMEM((width, tok_count), jnp.bfloat16),
        ),
        in_specs=[VMEM] * (len(normed) + 1),
        out_specs=(VMEM, VMEM),
        compiler_params=pltpu.CompilerParams(vmem_limit_bytes=KERNEL_VMEM),
        name="project",
    )(*normed, weight)


def grads_kernel(
    place_ref,
    projected_ref,
    normed_t_ref,
    cotangent_ref,
    theirs_ref,
    mine_ref,
    sums_ref,
    *,
    part,
):
    low = jnp.bfloat16
    tok_count, head_cols = cotangent_ref.shape
    width = normed_t_ref.shape[0]
    queries, key_rows, value_rows = projected_ref[0], projected_ref[1], projected_ref[2]
    half = tok_count // TP_OUTER
    first = place_ref[1] * part
    turn = jnp.where(first == 0, 0, half - first)
    upstream = cotangent_ref[...].astype(jnp.float32)
    upstream = jnp.concatenate(
        [pltpu.roll(upstream[i * half : (i + 1) * half], turn, 0) for i in range(TP_OUTER)], 0
    ).astype(low)
    zero = jnp.zeros((), low)
    score_scale = jnp.asarray(HD ** (-0.5), low)
    keys_t = key_rows.T
    grad_values, grad_keys, grad_queries = [], [], []
    for head in range(head_cols // HD):
        own = head_mask(queries.shape, head)
        q = jnp.where(own, queries, zero)
        g = jnp.where(own, upstream, zero)
        scores = dot(key_rows, q * score_scale, NT)
        weights = jnp.exp(scores - jnp.max(scores, axis=0, keepdims=True))
        attention = weights * (1.0 / jnp.sum(weights, axis=0, keepdims=True))
        grad_attention = dot(value_rows, g * score_scale, NT)
        mean = jnp.sum(attention * grad_attention, axis=0, keepdims=True)
        scaled = (attention * (grad_attention - mean)).astype(low)
        grad_values.append(dot(attention.astype(low), g))
        grad_keys.append(dot(scaled, q))
        grad_queries.append(dot(keys_t[head * HD : (head + 1) * HD], scaled))
    normed_t = normed_t_ref[...]
    joined = (
        jnp.concatenate(grad_queries, 0).astype(low).T,
        sum(grad_keys).astype(low),
        sum(grad_values).astype(low),
    )
    for c, grad in enumerate(joined):
        sums_ref[pl.ds(c * width, width), :] = dot(normed_t, grad)
    core = place_ref[0]
    rows = theirs_ref.shape[1]
    for outer in range(GRP_OUTER):
        own = pl.multiple_of((outer * GRP_INNER + core) * rows, rows)
        other = pl.multiple_of((outer * GRP_INNER + 1 - core) * rows, rows)
        mine_ref[outer] = sums_ref[pl.ds(own, rows), :]
        theirs_ref[outer] = sums_ref[pl.ds(other, rows), :].astype(low)


def weight_partials(place, projected, normed_t, cotangent, part):
    width, head_cols = normed_t.shape[0], cotangent.shape[1]
    half = (GRP_OUTER, 3 * width // (GRP_OUTER * GRP_INNER), head_cols)
    return pl.pallas_call(
        functools.partial(grads_kernel, part=part),
        out_shape=(
            pltpu.VMEM(half, jnp.bfloat16),
            pltpu.VMEM(half, jnp.float32),
        ),
        in_specs=[SMEM, VMEM, VMEM, VMEM],
        out_specs=(VMEM, VMEM),
        scratch_shapes=[pltpu.VMEM((3 * width, head_cols), jnp.float32)],
        compiler_params=pltpu.CompilerParams(vmem_limit_bytes=KERNEL_VMEM),
        name="grads",
    )(place, projected, normed_t, cotangent)


def make_body(seq_size):
    def body(crops, dout, crop_count, crop_ids, seq_slot, norm_gain, qkv_weight):
        return step(crops, dout, crop_count, crop_ids, seq_slot, norm_gain, qkv_weight)

    def step(crops, dout, crop_count, crop_ids, seq_slot, norm_gain, qkv_weight):
        tok_local, _ = crops.shape[2:]
        tok_count, head_cols = dout.shape[2:]
        tp_inner = tok_count // tok_local // TP_OUTER
        chunk = tok_count // seq_size

        pieces = lax.all_to_all(
            dout[0, 0].reshape(seq_size, chunk, head_cols), "z", 0, 0, tiled=True
        )
        routed = by_candidate(crop_count, crop_ids, seq_slot, near(pieces))
        cotangent = lax.all_to_all(routed, "z", 0, 0, tiled=True)
        cotangent = cotangent.reshape(tok_count, head_cols)

        local = layer_norm(crops[0, 0], norm_gain)
        both = lax.all_gather(local, "yl", axis=0, tiled=True)
        normed = [near(both)]
        for d in range(1, tp_inner):
            pairs = [(i, (i - d) % tp_inner) for i in range(tp_inner)]
            normed.append(near(lax.ppermute(both, "x", pairs)))

        kept = project(normed, qkv_weight)
        place = jnp.stack([lax.axis_index("core"), lax.axis_index("x")])
        theirs, mine = weight_partials(
            place, *[near(value) for value in kept], near(cotangent), tok_local
        )

        received = lax.ppermute(theirs, "core", [(0, 1), (1, 0)])
        total = (mine + received.astype(jnp.float32)).astype(jnp.bfloat16)
        total = total.reshape(GRP_OUTER * seq_size, -1, head_cols)
        parts = lax.all_to_all(total, ("yh", "z"), 0, 0, tiled=True)
        return jnp.sum(parts.astype(jnp.float32), axis=0)

    return body


def solution(mesh):
    seq_size = mesh.shape["seq"]
    tp_inner = mesh.shape["tp"] // TP_OUTER
    fine = Mesh(
        mesh.devices.reshape(GRP_OUTER, GRP_INNER, TP_OUTER, tp_inner, seq_size),
        ("yh", "core", "yl", "x", "z"),
    )
    grp, tp = ("yh", "core"), ("yl", "x")
    in_specs = (
        P(grp, "z", tp, None),
        P(grp, "z", None, tp),
        P(grp),
        P(grp, None),
        P(grp, None),
        P(),
        P(None, None, tp),
    )
    out_specs = P((*grp, "z"), tp)
    return jax.shard_map(
        make_body(seq_size), mesh=fine, in_specs=in_specs, out_specs=out_specs, check_vma=False
    )
```
